128 devices in a mesh: section: 16 (over z, x_lo, core), tensor: 8 (over x_hi, y).
Axes of the slice: x: 4 (x_hi: 2, x_lo: 2; x = x_hi * 2 + x_lo), y: 4, z: 4, core: 2. Of those that a mesh axis runs over, the one named last changes fastest.
Arguments:
- fwd_input: float32 [16, 256, 1024], P('section', 'tensor'), may hold values from -6 to 6
- out_grad: float32 [16, 256, 1024], P('section', 'tensor'), may hold values from -6 to 6
- w_inner: float32 [16, 1024, 16384], P('section', None, 'tensor'), may hold values from -0.1875 to 0.1875
- w_outer: float32 [16, 16384, 1024], P('section', 'tensor'), may hold values from -0.046875 to 0.046875
- lent_saved: float32 [16, 256, 16384], P('section', None, 'tensor'), may hold values from -6 to 6
Outputs:
- fwd_output: float32 [16, 256, 1024], P('section', 'tensor')
- in_grad: float32 [16, 256, 1024], P('section', 'tensor')
- lent_new: float32 [16, 256, 16384], P('section', None, 'tensor')
The draws below stay inside these ranges and needn't reach their ends.
All inputs are finite; a program needn't handle non-finite values.
Results may differ from the reference program's by a relative error of at most 0.00007.
Values sent between devices are 32-bit elements; how exact they have to be, the bound alone decides.
No kernel may reach another device: no remote copies, remote signals or barrier semaphores. Data moves between devices by JAX's collectives and lax.ppermute only.
A program may use at most 128 MiB of HBM per device.

```python
import jax
import jax.numpy as jnp
from jax import lax

D = 1024
FF = 16384
ROWS = 256
SECTIONS = 16
HALF = 8


def level_of(own_key, dims, shards, smallest, largest):
    def one(position, parts):
        steps = jax.random.uniform(jax.random.fold_in(jax.random.fold_in(own_key, 6), position), (parts,), jnp.float32, smallest / len(shards), largest / len(shards))
        return jnp.repeat(jnp.exp(steps), dims[position] // parts).reshape((-1,) + (1,) * (len(dims) - position - 1))

    gain = one(*shards[0])
    for cut in shards[1:]:
        gain = gain * one(*cut)
    return gain


def bell_draw(own_key, shape, scale, reach, shards=(), kind=jnp.bfloat16):
    loudness = level_of(own_key, shape, shards, -0.22, 0.18) if shards else 1.0
    entries = jax.random.normal(own_key, shape, jnp.float32) * scale * loudness
    return jnp.minimum(jnp.maximum(entries, -reach), reach).astype(kind)


def setup_inputs(seed: int = 0) -> dict:
    streams_of = jax.random.split(jax.random.key(seed), 6)
    return {
        "fwd_input": bell_draw(streams_of[0], (SECTIONS, ROWS, D), 1.0, 6.0, ((0, 16), (1, 8)), jnp.float32),
        "out_grad": bell_draw(streams_of[1], (SECTIONS, ROWS, D), 1.0, 6.0, ((0, 16), (1, 8)), jnp.float32),
        "w_inner": bell_draw(streams_of[2], (SECTIONS, D, FF), D ** -0.5, 0.1875, ((0, 16), (2, 8)), jnp.float32),
        "w_outer": bell_draw(streams_of[3], (SECTIONS, FF, D), FF ** -0.5, 0.046875, ((0, 16), (1, 8)), jnp.float32),
        "lent_saved": bell_draw(streams_of[4], (SECTIONS, ROWS, FF), 1.0, 6.0, ((0, 16), (2, 8)), jnp.float32),
    }


def gelu_exact(value):
    return 0.5 * value * (1.0 + jax.scipy.special.erf(value / jnp.sqrt(2.0).astype(value.dtype)))

def gelu_slope(value):
    cumul = 0.5 * (1.0 + jax.scipy.special.erf(value / jnp.sqrt(2.0).astype(value.dtype)))
    dense = jnp.exp(-0.5 * value * value) / jnp.sqrt(2.0 * jnp.pi).astype(value.dtype)
    return cumul + value * dense

def one_layer(items):
    x_rows, g_rows, w_first, w_second, old_pre = items
    hi = lax.Precision.HIGHEST
    pre = jnp.dot(x_rows, w_first, precision=hi, preferred_element_type=jnp.float32)
    out = x_rows + jnp.dot(gelu_exact(pre), w_second, precision=hi, preferred_element_type=jnp.float32)
    d_act = lax.dot_general(g_rows, w_second, (((1,), (1,)), ((), ())), precision=hi, preferred_element_type=jnp.float32)
    d_pre = d_act * gelu_slope(old_pre)
    grad = g_rows + lax.dot_general(d_pre, w_first, (((1,), (1,)), ((), ())), precision=hi, preferred_element_type=jnp.float32)
    return (out, grad, pre)

def reference(fwd_input, out_grad, w_inner, w_outer, lent_saved):
    old_pre = jnp.roll(lent_saved, -HALF, axis=0)
    outs, grads, pres = lax.map(one_layer, (fwd_input, out_grad, w_inner, w_outer, old_pre))
    fwd_output = jnp.roll(outs, 1, axis=0)
    in_grad = jnp.roll(grads, -1, axis=0)
    lent_new = jnp.roll(pres, -HALF, axis=0)
    return (fwd_output, in_grad, lent_new)
```

```python
import functools
import math

import jax
import jax.numpy as jnp
from jax import lax
from jax.experimental import pallas as pl
from jax.experimental.pallas import tpu as pltpu
from jax.sharding import PartitionSpec as P

F32 = jnp.float32
BF16 = jnp.bfloat16
ROOT_HALF = math.sqrt(0.5)
DENSITY = 1.0 / math.sqrt(2.0 * math.pi)
VMEM_LIMIT = 48 * 1024 * 1024


def shifted(value, by):
    length = lax.axis_size("section")
    return lax.ppermute(value, "section", [(i, (i + by) % length) for i in range(length)])


def across(value, mask):
    length = lax.axis_size("tensor")
    return lax.ppermute(value, "tensor", [(i, i ^ mask) for i in range(length)])


def halves(value):
    high = value.astype(BF16)
    return high, (value - high.astype(F32)).astype(BF16)


def product(left, right, contract):
    dims = (contract, ((), ()))
    (lh, ll), (rh, rl) = left, right
    dot = functools.partial(lax.dot_general, dimension_numbers=dims, preferred_element_type=F32)
    return dot(lh, rh) + (dot(lh, rl) + dot(ll, rh))


PLAIN = ((1,), (0,))
TURNED = ((1,), (1,))


def gelu(value):
    return 0.5 * value * (1.0 + lax.erf(value * ROOT_HALF))


def gelu_slope(value):
    return 0.5 * (1.0 + lax.erf(value * ROOT_HALF)) + value * (jnp.exp(-0.5 * value * value) * DENSITY)


def forward_kernel(parts, rows, *refs):
    place_ref, refs = refs[0], refs[1:]
    got, refs = refs[:parts], refs[parts:]
    first_ref, second_ref, pre_ref, dact_ref, sum_ref, xh, xl, gh, gl = refs

    @pl.when(pl.program_id(0) == 0)
    def _():
        place = place_ref[0]
        for mask in range(parts):
            at = pl.ds(pl.multiple_of((place ^ mask) * rows, rows), rows)
            high, low = halves(got[mask][:rows])
            xh[at, :] = high
            xl[at, :] = low
            high, low = halves(got[mask][rows:])
            gh[at, :] = high
            gl[at, :] = low
        sum_ref[...] = jnp.zeros_like(sum_ref)

    pre = product((xh[...], xl[...]), halves(first_ref[...]), PLAIN)
    pre_ref[...] = pre
    second = halves(second_ref[...])
    dact_ref[...] = product((gh[...], gl[...]), second, TURNED)
    sum_ref[...] += product(halves(gelu(pre)), second, PLAIN)


def forward(place, got, w_first, w_second, tile):
    parts, rows, depth = len(got), got[0].shape[0] // 2, got[0].shape[1]
    hidden = w_first.shape[1]
    total = parts * rows
    whole = pl.BlockSpec((2 * rows, depth), lambda j, s: (0, 0))
    column = pl.BlockSpec((total, tile), lambda j, s: (0, j))
    return pl.pallas_call(
        functools.partial(forward_kernel, parts, rows),
        out_shape=(
            jax.ShapeDtypeStruct((total, hidden), F32),
            jax.ShapeDtypeStruct((total, hidden), F32),
            jax.ShapeDtypeStruct((total, depth), F32),
        ),
        grid_spec=pltpu.PrefetchScalarGridSpec(
            num_scalar_prefetch=1,
            grid=(hidden // tile,),
            in_specs=[whole] * parts
            + [
                pl.BlockSpec((depth, tile), lambda j, s: (0, j)),
                pl.BlockSpec((tile, depth), lambda j, s: (j, 0)),
            ],
            out_specs=[column, column, pl.BlockSpec((total, depth), lambda j, s: (0, 0))],
            scratch_shapes=[pltpu.VMEM((total, depth), BF16)] * 4,
        ),
        compiler_params=pltpu.CompilerParams(
            dimension_semantics=("arbitrary",), vmem_limit_bytes=VMEM_LIMIT
        ),
        cost_estimate=pl.CostEstimate(
            flops=18 * total * depth * hidden,
            bytes_accessed=4 * (2 * depth * hidden + 2 * total * hidden + 3 * total * depth),
            transcendentals=total * hidden,
        ),
        name="forward",
    )(place, *got, w_first, w_second)


def backward_kernel(parts, rows, *refs):
    place_ref, dact_ref, old_ref, first_ref, fsum_ref = refs[:5]
    outs, acc = refs[5 : 5 + parts], refs[5 + parts]

    @pl.when(pl.program_id(0) == 0)
    def _():
        acc[...] = jnp.zeros_like(acc)

    hidden_grad = dact_ref[...] * gelu_slope(old_ref[...])
    acc[...] += product(halves(hidden_grad), halves(first_ref[...]), TURNED)

    @pl.when(pl.program_id(0) == pl.num_programs(0) - 1)
    def _():
        place = place_ref[0]
        for mask in range(parts):
            at = pl.ds(pl.multiple_of((place ^ mask) * rows, rows), rows)
            outs[mask][:rows] = fsum_ref[at, :]
            outs[mask][rows:] = acc[at, :]


def backward(place, d_act, old_pre, w_first, fwd_sum, parts, tile):
    total, hidden = d_act.shape
    depth = w_first.shape[0]
    rows = total // parts
    column = pl.BlockSpec((total, tile), lambda j, s: (0, j))
    return pl.pallas_call(
        functools.partial(backward_kernel, parts, rows),
        out_shape=[jax.ShapeDtypeStruct((2 * rows, depth), F32)] * parts,
        grid_spec=pltpu.PrefetchScalarGridSpec(
            num_scalar_prefetch=1,
            grid=(hidden // tile,),
            in_specs=[
                column,
                column,
                pl.BlockSpec((depth, tile), lambda j, s: (0, j)),
                pl.BlockSpec((total, depth), lambda j, s: (0, 0)),
            ],
            out_specs=[pl.BlockSpec((2 * rows, depth), lambda j, s: (0, 0))] * parts,
            scratch_shapes=[pltpu.VMEM((total, depth), F32)],
        ),
        compiler_params=pltpu.CompilerParams(
            dimension_semantics=("arbitrary",), vmem_limit_bytes=VMEM_LIMIT
        ),
        cost_estimate=pl.CostEstimate(
            flops=6 * total * depth * hidden,
            bytes_accessed=4 * (depth * hidden + 2 * total * hidden + 3 * total * depth),
            transcendentals=2 * total * hidden,
        ),
        name="backward",
    )(place, d_act, old_pre, w_first, fwd_sum)


def shards(fwd_input, out_grad, w_inner, w_outer, lent_saved):
    parts = lax.axis_size("tensor")
    half = lax.axis_size("section") // 2
    rows = fwd_input.shape[1]
    place = lax.axis_index("tensor").astype(jnp.int32)[None]

    old_pre = shifted(lent_saved[0], half)
    both = jnp.concatenate([fwd_input[0], out_grad[0]], axis=0)
    got = [both] + [across(both, mask) for mask in range(1, parts)]
    pre, d_act, fwd_sum = forward(place, got, w_inner[0], w_outer[0], 256)
    given = shifted(pre, half)
    sums = backward(place, d_act, old_pre, w_inner[0], fwd_sum, parts, 256)
    total = both + sums[0]
    for mask in range(1, parts):
        total = total + across(sums[mask], mask)
    moved_out = shifted(total[:rows], 1)
    moved_grad = shifted(total[rows:], -1)
    return (moved_out[None], moved_grad[None], given[None])


def solution(mesh):
    return jax.shard_map(
        shards,
        mesh=mesh,
        in_specs=(
            P("section", "tensor", None),
            P("section", "tensor", None),
            P("section", None, "tensor"),
            P("section", "tensor", None),
            P("section", None, "tensor"),
        ),
        out_specs=(
            P("section", "tensor", None),
            P("section", "tensor", None),
            P("section", None, "tensor"),
        ),
        check_vma=False,
    )
```

```python
import functools
import math

import jax
import jax.numpy as jnp
from jax import lax
from jax.experimental import pallas as pl
from jax.experimental.pallas import tpu as pltpu
from jax.sharding import PartitionSpec as P

F32 = jnp.float32
BF16 = jnp.bfloat16
ROOT_HALF = math.sqrt(0.5)
DENSITY = 1.0 / math.sqrt(2.0 * math.pi)
COST = {"pre": 10**3, "dact": 10**3, "out": 10**3, "back": 10**12}
VMEM_LIMIT = 48 * 1024 * 1024


def shifted(value, by):
    length = lax.axis_size("section")
    return lax.ppermute(value, "section", [(i, (i + by) % length) for i in range(length)])


def across(value, mask):
    length = lax.axis_size("tensor")
    return lax.ppermute(value, "tensor", [(i, i ^ mask) for i in range(length)])


def halves(value):
    high = value.astype(BF16)
    return high, (value - high.astype(F32)).astype(BF16)


def product(left, right, contract):
    dims = (contract, ((), ()))
    (lh, ll), (rh, rl) = left, right
    dot = functools.partial(lax.dot_general, dimension_numbers=dims, preferred_element_type=F32)
    return dot(lh, rh) + (dot(lh, rl) + dot(ll, rh))


PLAIN = ((1,), (0,))
TURNED = ((1,), (1,))


def gelu(value):
    return 0.5 * value * (1.0 + lax.erf(value * ROOT_HALF))


def gelu_slope(value):
    return 0.5 * (1.0 + lax.erf(value * ROOT_HALF)) + value * (jnp.exp(-0.5 * value * value) * DENSITY)


def assemble(place_ref, pairs, high_ref, low_ref):
    rows = pairs[0].shape[0] // 2
    for mask in range(2 * len(pairs)):
        at = pl.ds(pl.multiple_of((place_ref[0] ^ mask) * rows, rows), rows)
        start = mask // len(pairs) * rows
        high_ref[at, :], low_ref[at, :] = halves(pairs[mask % len(pairs)][start : start + rows])


def in_kernel(contract, place_ref, *refs):
    *pairs, weight_ref, result_ref, high, low = refs

    @pl.when(pl.program_id(0) == 0)
    def _():
        assemble(place_ref, pairs, high, low)

    result_ref[...] = product((high[...], low[...]), halves(weight_ref[...]), contract)


def out_kernel(pre_ref, second_ref, sum_ref):
    @pl.when(pl.program_id(0) == 0)
    def _():
        sum_ref[...] = jnp.zeros_like(sum_ref)

    sum_ref[...] += product(halves(gelu(pre_ref[...])), halves(second_ref[...]), PLAIN)


def back_kernel(dact_ref, old_ref, first_ref, sum_ref):
    @pl.when(pl.program_id(0) == 0)
    def _():
        sum_ref[...] = jnp.zeros_like(sum_ref)

    hidden_grad = dact_ref[...] * gelu_slope(old_ref[...])
    sum_ref[...] += product(halves(hidden_grad), halves(first_ref[...]), TURNED)


def kernel_call(body, name, tile, inputs, kinds, outputs, scratch, products=1):
    def spec(shape, kind):
        if kind == "scalar":
            return pl.BlockSpec(memory_space=pltpu.SMEM)
        if kind == "column":
            return pl.BlockSpec((shape[0], tile), lambda j: (0, j))
        if kind == "row":
            return pl.BlockSpec((tile, shape[1]), lambda j: (j, 0))
        return pl.BlockSpec(shape, lambda j: (0, 0))

    shapes = [value.shape for value in inputs]
    hidden, depth = max(shapes[-1]), min(shapes[-1])
    rows = outputs[0][0][0]
    moved = sum(4 * math.prod(shape) for shape in shapes + [shape for shape, _ in outputs])
    return pl.pallas_call(
        body,
        grid=(hidden // tile,),
        out_shape=[jax.ShapeDtypeStruct(shape, F32) for shape, _ in outputs],
        in_specs=[spec(shape, kind) for shape, kind in zip(shapes, kinds)],
        out_specs=[spec(shape, kind) for shape, kind in outputs],
        scratch_shapes=scratch,
        compiler_params=pltpu.CompilerParams(
            dimension_semantics=("arbitrary",), vmem_limit_bytes=VMEM_LIMIT
        ),
        cost_estimate=pl.CostEstimate(
            flops=COST[name], bytes_accessed=1000, transcendentals=0
        ),
        name=name,
    )(*inputs)


def exchanged(value):
    return lax.all_to_all(value, "tensor", 0, 0, tiled=True)


def scattered(rows, value):
    return rows + jnp.sum(exchanged(value).reshape(-1, *rows.shape), axis=0)


def shards(fwd_input, out_grad, w_inner, w_outer, lent_saved):
    half = lax.axis_size("section") // 2
    parts = lax.axis_size("tensor")
    place = lax.axis_index("tensor").astype(jnp.int32)[None]
    x_rows, g_rows, w_first, w_second = fwd_input[0], out_grad[0], w_inner[0], w_outer[0]

    old_pre = shifted(lent_saved[0], half)
    total, depth = parts * x_rows.shape[0], x_rows.shape[1]
    wide, narrow = (total, w_first.shape[1]), (total, depth)
    scratch = [pltpu.VMEM(narrow, BF16)] * 2

    def gathered(rows):
        pair = jnp.concatenate([rows, across(rows, parts // 2)])
        return [pair] + [across(pair, mask) for mask in range(1, parts // 2)]

    x_pairs, g_pairs = gathered(x_rows), gathered(g_rows)
    kinds = ["scalar"] + [""] * len(x_pairs)
    (pre,) = kernel_call(
        functools.partial(in_kernel, PLAIN), "pre", 512, [place, *x_pairs, w_first], kinds + ["column"],
        [(wide, "column")], scratch,
    )
    given = shifted(pre, half)
    (d_act,) = kernel_call(
        functools.partial(in_kernel, TURNED), "dact", 512, [place, *g_pairs, w_second], kinds + ["row"],
        [(wide, "column")], scratch,
    )
    (fwd_sum,) = kernel_call(out_kernel, "out", 512, [pre, w_second], ["column", "row"], [(narrow, "")], [])
    moved_out = shifted(scattered(x_rows, fwd_sum), 1)
    (bwd_sum,) = kernel_call(
        back_kernel, "back", 512, [d_act, old_pre, w_first], ["column", "column", "column"], [(narrow, "")], []
    )
    moved_grad = shifted(scattered(g_rows, bwd_sum), -1)
    return (moved_out[None], moved_grad[None], given[None])


def solution(mesh):
    return jax.shard_map(
        shards,
        mesh=mesh,
        in_specs=(
            P("section", "tensor", None),
            P("section", "tensor", None),
            P("section", None, "tensor"),
            P("section", "tensor", None),
            P("section", None, "tensor"),
        ),
        out_specs=(
            P("section", "tensor", None),
            P("section", "tensor", None),
            P("section", None, "tensor"),
        ),
        check_vma=False,
    )
```

```python
import functools
import math

import jax
import jax.numpy as jnp
from jax import lax
from jax.experimental import pallas as pl
from jax.experimental.pallas import tpu as pltpu
from jax.sharding import PartitionSpec as P

F32 = jnp.float32
BF16 = jnp.bfloat16
ROOT_HALF = math.sqrt(0.5)
DENSITY = 1.0 / math.sqrt(2.0 * math.pi)
COST = {"pre": 10**3, "dact": 10**3, "out": 10**3, "back": 10**12}
VMEM_LIMIT = 48 * 1024 * 1024


def shifted(value, by):
    length = lax.axis_size("section")
    return lax.ppermute(value, "section", [(i, (i + by) % length) for i in range(length)])


def across(value, mask):
    length = lax.axis_size("tensor")
    return lax.ppermute(value, "tensor", [(i, i ^ mask) for i in range(length)])


def halves(value):
    high = value.astype(BF16)
    return high, (value - high.astype(F32)).astype(BF16)


def product(left, right, contract):
    dims = (contract, ((), ()))
    (lh, ll), (rh, rl) = left, right
    dot = functools.partial(lax.dot_general, dimension_numbers=dims, preferred_element_type=F32)
    return dot(lh, rh) + (dot(lh, rl) + dot(ll, rh))


PLAIN = ((1,), (0,))
TURNED = ((1,), (1,))


def gelu(value):
    return 0.5 * value * (1.0 + lax.erf(value * ROOT_HALF))


def gelu_slope(value):
    return 0.5 * (1.0 + lax.erf(value * ROOT_HALF)) + value * (jnp.exp(-0.5 * value * value) * DENSITY)


def assemble(place_ref, pairs, high_ref, low_ref):
    rows = pairs[0].shape[0] // 2
    for mask in range(2 * len(pairs)):
        at = pl.ds(pl.multiple_of((place_ref[0] ^ mask) * rows, rows), rows)
        start = mask // len(pairs) * rows
        high_ref[at, :], low_ref[at, :] = halves(pairs[mask % len(pairs)][start : start + rows])


def in_kernel(contract, place_ref, *refs):
    pairs, weight_ref, results, (high, low) = refs[:4], refs[4], refs[5:-2], refs[-2:]

    @pl.when(pl.program_id(0) == 0)
    def _():
        assemble(place_ref, pairs, high, low)

    result = product((high[...], low[...]), halves(weight_ref[...]), contract)
    start = 0
    for ref in results:
        ref[...] = result[start : start + ref.shape[0]]
        start += ref.shape[0]


def out_kernel(*refs):
    *pres, second_ref, sum_ref = refs

    @pl.when(pl.program_id(0) == 0)
    def _():
        sum_ref[...] = jnp.zeros_like(sum_ref)

    act = jnp.concatenate([gelu(ref[...]) for ref in pres])
    sum_ref[...] += product(halves(act), halves(second_ref[...]), PLAIN)


def back_kernel(dact_ref, old_ref, first_ref, sum_ref):
    @pl.when(pl.program_id(0) == 0)
    def _():
        sum_ref[...] = jnp.zeros_like(sum_ref)

    hidden_grad = dact_ref[...] * gelu_slope(old_ref[...])
    sum_ref[...] += product(halves(hidden_grad), halves(first_ref[...]), TURNED)


def kernel_call(body, name, tile, inputs, kinds, outputs, scratch, products=1):
    def spec(shape, kind):
        if kind == "scalar":
            return pl.BlockSpec(memory_space=pltpu.SMEM)
        if kind == "column":
            return pl.BlockSpec((shape[0], tile), lambda j: (0, j))
        if kind == "row":
            return pl.BlockSpec((tile, shape[1]), lambda j: (j, 0))
        return pl.BlockSpec(shape, lambda j: (0, 0))

    shapes = [value.shape for value in inputs]
    hidden, depth = max(shapes[-1]), min(shapes[-1])
    rows = outputs[0][0][0]
    moved = sum(4 * math.prod(shape) for shape in shapes + [shape for shape, _ in outputs])
    return pl.pallas_call(
        body,
        grid=(hidden // tile,),
        out_shape=[jax.ShapeDtypeStruct(shape, F32) for shape, _ in outputs],
        in_specs=[spec(shape, kind) for shape, kind in zip(shapes, kinds)],
        out_specs=[spec(shape, kind) for shape, kind in outputs],
        scratch_shapes=scratch,
        compiler_params=pltpu.CompilerParams(
            dimension_semantics=("arbitrary",), vmem_limit_bytes=VMEM_LIMIT
        ),
        cost_estimate=pl.CostEstimate(
            flops=COST[name], bytes_accessed=1000, transcendentals=0
        ),
        name=name,
    )(*inputs)


def exchanged(value):
    return lax.all_to_all(value, "tensor", 0, 0, tiled=True)


def copy_all(pairs, sems):
    copies = [pltpu.make_async_copy(source, target, sems.at[i]) for i, (source, target) in enumerate(pairs)]
    for copy in copies:
        copy.start()
    for copy in copies:
        copy.wait()


ANYWHERE = pl.BlockSpec(memory_space=pl.ANY)


def placed(total, upper, *others):
    def body(upper_ref, *refs):
        sources, lent_ref, targets, sems = refs[: len(others)], refs[len(others)], refs[len(others) + 1 : -1], refs[-1]
        copy_all([(upper_ref, lent_ref.at[pl.ds(0, upper.shape[0])]), *zip(sources, targets)], sems)

    return pl.pallas_call(
        body,
        out_shape=[jax.ShapeDtypeStruct((total, upper.shape[1]), F32)]
        + [jax.ShapeDtypeStruct(value.shape, F32) for value in others],
        in_specs=[pl.BlockSpec(memory_space=pltpu.VMEM)] * (1 + len(others)),
        out_specs=[ANYWHERE] * (1 + len(others)),
        scratch_shapes=[pltpu.SemaphoreType.DMA((1 + len(others),))],
        name="placed",
    )(upper, *others)


def scattered(rows, value):
    return rows + jnp.sum(exchanged(value).reshape(-1, *rows.shape), axis=0)


def shards(fwd_input, out_grad, w_inner, w_outer, lent_saved):
    half = lax.axis_size("section") // 2
    parts = lax.axis_size("tensor")
    place = lax.axis_index("tensor").astype(jnp.int32)[None]
    x_rows, g_rows, w_first, w_second = fwd_input[0], out_grad[0], w_inner[0], w_outer[0]

    old_pre = shifted(lent_saved[0], half)
    total, depth = parts * x_rows.shape[0], x_rows.shape[1]
    wide, narrow = (total, w_first.shape[1]), (total, depth)
    scratch = [pltpu.VMEM(narrow, BF16)] * 2
    last = total // 8

    def gathered(rows):
        pair = jnp.concatenate([rows, across(rows, parts // 2)])
        return [pair] + [across(pair, mask) for mask in range(1, parts // 2)]

    x_pairs, g_pairs = gathered(x_rows), gathered(g_rows)
    kinds = ["scalar"] + [""] * len(x_pairs)
    pres = kernel_call(
        functools.partial(in_kernel, PLAIN), "pre", 512, [place, *x_pairs, w_first], kinds + ["column"],
        [((count, wide[1]), "column") for count in (total - last, last)], scratch,
    )
    given = [shifted(pre, half) for pre in pres]
    (d_act,) = kernel_call(
        functools.partial(in_kernel, TURNED), "dact", 512, [place, *g_pairs, w_second], kinds + ["row"],
        [(wide, "column")], scratch,
    )
    (fwd_sum,) = kernel_call(out_kernel, "out", 512, [*pres, w_second], ["column"] * len(pres) + ["row"], [(narrow, "")], [])
    moved_out = shifted(scattered(x_rows, fwd_sum), 1)
    (bwd_sum,) = kernel_call(
        back_kernel, "back", 512, [d_act, old_pre, w_first], ["column", "column", "column"], [(narrow, "")], []
    )
    moved_grad = shifted(scattered(g_rows, bwd_sum), -1)
    lent, moved_out, moved_grad = placed(total, given[0], moved_out, moved_grad)
    lent = lax.dynamic_update_slice(lent, given[1], (total - last, 0))
    return (moved_out[None], moved_grad[None], lent[None])


def solution(mesh):
    return jax.shard_map(
        shards,
        mesh=mesh,
        in_specs=(
            P("section", "tensor", None),
            P("section", "tensor", None),
            P("section", None, "tensor"),
            P("section", "tensor", None),
            P("section", None, "tensor"),
        ),
        out_specs=(
            P("section", "tensor", None),
            P("section", "tensor", None),
            P("section", None, "tensor"),
        ),
        check_vma=False,
    )
```

```python
import functools
import math

import jax
import jax.numpy as jnp
from jax import lax
from jax.experimental import pallas as pl
from jax.experimental.pallas import tpu as pltpu
from jax.sharding import PartitionSpec as P

F32 = jnp.float32
BF16 = jnp.bfloat16
ROOT_HALF = math.sqrt(0.5)
DENSITY = 1.0 / math.sqrt(2.0 * math.pi)
COST = {"pre": 10**3, "dact": 10**3, "out": 10**3, "back": 10**12}
VMEM_LIMIT = 48 * 1024 * 1024


def shifted(value, by):
    length = lax.axis_size("section")
    return lax.ppermute(value, "section", [(i, (i + by) % length) for i in range(length)])


def across(value, mask):
    length = lax.axis_size("tensor")
    return lax.ppermute(value, "tensor", [(i, i ^ mask) for i in range(length)])


def halves(value):
    high = value.astype(BF16)
    return high, (value - high.astype(F32)).astype(BF16)


def product(left, right, contract):
    dims = (contract, ((), ()))
    (lh, ll), (rh, rl) = left, right
    dot = functools.partial(lax.dot_general, dimension_numbers=dims, preferred_element_type=F32)
    return dot(lh, rh) + (dot(lh, rl) + dot(ll, rh))


PLAIN = ((1,), (0,))
TURNED = ((1,), (1,))


def gelu(value):
    return 0.5 * value * (1.0 + lax.erf(value * ROOT_HALF))


def gelu_slope(value):
    return 0.5 * (1.0 + lax.erf(value * ROOT_HALF)) + value * (jnp.exp(-0.5 * value * value) * DENSITY)


def assemble(place_ref, pairs, high_ref, low_ref):
    rows = pairs[0].shape[0] // 2
    for mask in range(2 * len(pairs)):
        at = pl.ds(pl.multiple_of((place_ref[0] ^ mask) * rows, rows), rows)
        start = mask // len(pairs) * rows
        high_ref[at, :], low_ref[at, :] = halves(pairs[mask % len(pairs)][start : start + rows])


def in_kernel(contract, place_ref, *refs):
    pairs, weight_ref, results, (high, low) = refs[:4], refs[4], refs[5:-2], refs[-2:]

    @pl.when(pl.program_id(0) == 0)
    def _():
        assemble(place_ref, pairs, high, low)

    result = product((high[...], low[...]), halves(weight_ref[...]), contract)
    start = 0
    for ref in results:
        ref[...] = result[start : start + ref.shape[0]]
        start += ref.shape[0]


def out_kernel(*refs):
    *pres, second_ref, sum_ref = refs

    @pl.when(pl.program_id(0) == 0)
    def _():
        sum_ref[...] = jnp.zeros_like(sum_ref)

    act = jnp.concatenate([gelu(ref[...]) for ref in pres])
    sum_ref[...] += product(halves(act), halves(second_ref[...]), PLAIN)


def back_kernel(dact_ref, old_ref, first_ref, sum_ref):
    @pl.when(pl.program_id(0) == 0)
    def _():
        sum_ref[...] = jnp.zeros_like(sum_ref)

    hidden_grad = dact_ref[...] * gelu_slope(old_ref[...])
    sum_ref[...] += product(halves(hidden_grad), halves(first_ref[...]), TURNED)


def kernel_call(body, name, tile, inputs, kinds, outputs, scratch, products=1):
    def spec(shape, kind):
        if kind == "scalar":
            return pl.BlockSpec(memory_space=pltpu.SMEM)
        if kind == "column":
            return pl.BlockSpec((shape[0], tile), lambda j: (0, j))
        if kind == "row":
            return pl.BlockSpec((tile, shape[1]), lambda j: (j, 0))
        return pl.BlockSpec(shape, lambda j: (0, 0))

    shapes = [value.shape for value in inputs]
    hidden, depth = max(shapes[-1]), min(shapes[-1])
    rows = outputs[0][0][0]
    moved = sum(4 * math.prod(shape) for shape in shapes + [shape for shape, _ in outputs])
    return pl.pallas_call(
        body,
        grid=(hidden // tile,),
        out_shape=[jax.ShapeDtypeStruct(shape, F32) for shape, _ in outputs],
        in_specs=[spec(shape, kind) for shape, kind in zip(shapes, kinds)],
        out_specs=[spec(shape, kind) for shape, kind in outputs],
        scratch_shapes=scratch,
        compiler_params=pltpu.CompilerParams(
            dimension_semantics=("arbitrary",), vmem_limit_bytes=VMEM_LIMIT
        ),
        cost_estimate=pl.CostEstimate(
            flops=COST[name], bytes_accessed=1000, transcendentals=0
        ),
        name=name,
    )(*inputs)


def exchanged(value):
    return lax.all_to_all(value, "tensor", 0, 0, tiled=True)


def copy_all(pairs, sems):
    copies = [pltpu.make_async_copy(source, target, sems.at[i]) for i, (source, target) in enumerate(pairs)]
    for copy in copies:
        copy.start()
    for copy in copies:
        copy.wait()


ANYWHERE = pl.BlockSpec(memory_space=pl.ANY)


def placed(total, upper, *others):
    def body(upper_ref, *refs):
        sources, lent_ref, targets, sems = refs[: len(others)], refs[len(others)], refs[len(others) + 1 : -1], refs[-1]
        copy_all([(upper_ref, lent_ref.at[pl.ds(0, upper.shape[0])]), *zip(sources, targets)], sems)

    return pl.pallas_call(
        body,
        out_shape=[jax.ShapeDtypeStruct((total, upper.shape[1]), F32)]
        + [jax.ShapeDtypeStruct(value.shape, F32) for value in others],
        in_specs=[pl.BlockSpec(memory_space=pltpu.VMEM)] * (1 + len(others)),
        out_specs=[ANYWHERE] * (1 + len(others)),
        scratch_shapes=[pltpu.SemaphoreType.DMA((1 + len(others),))],
        compiler_params=pltpu.CompilerParams(vmem_limit_bytes=8 * 1024 * 1024),
        name="placed",
    )(upper, *others)


def scattered(rows, value):
    return rows + jnp.sum(exchanged(value).reshape(-1, *rows.shape), axis=0)


def shards(fwd_input, out_grad, w_inner, w_outer, lent_saved):
    half = lax.axis_size("section") // 2
    parts = lax.axis_size("tensor")
    place = lax.axis_index("tensor").astype(jnp.int32)[None]
    x_rows, g_rows, w_first, w_second = fwd_input[0], out_grad[0], w_inner[0], w_outer[0]

    old_pre = shifted(lent_saved[0], half)
    total, depth = parts * x_rows.shape[0], x_rows.shape[1]
    wide, narrow = (total, w_first.shape[1]), (total, depth)
    scratch = [pltpu.VMEM(narrow, BF16)] * 2
    last = total // 8

    def gathered(rows):
        pair = jnp.concatenate([rows, across(rows, parts // 2)])
        return [pair] + [across(pair, mask) for mask in range(1, parts // 2)]

    x_pairs, g_pairs = gathered(x_rows), gathered(g_rows)
    kinds = ["scalar"] + [""] * len(x_pairs)
    pres = kernel_call(
        functools.partial(in_kernel, PLAIN), "pre", 512, [place, *x_pairs, w_first], kinds + ["column"],
        [((count, wide[1]), "column") for count in (total - last, last)], scratch,
    )
    given = [shifted(pre, half) for pre in pres]
    (d_act,) = kernel_call(
        functools.partial(in_kernel, TURNED), "dact", 512, [place, *g_pairs, w_second], kinds + ["row"],
        [(wide, "column")], scratch,
    )
    (fwd_sum,) = kernel_call(out_kernel, "out", 512, [*pres, w_second], ["column"] * len(pres) + ["row"], [(narrow, "")], [])
    moved_out = shifted(scattered(x_rows, fwd_sum), 1)
    (bwd_sum,) = kernel_call(
        back_kernel, "back", 512, [d_act, old_pre, w_first], ["column", "column", "column"], [(narrow, "")], []
    )
    moved_grad = shifted(scattered(g_rows, bwd_sum), -1)
    lent, moved_out, moved_grad = placed(total, given[0], moved_out, moved_grad)
    lent = lax.dynamic_update_slice(lent, given[1], (total - last, 0))
    return (moved_out[None], moved_grad[None], lent[None])


def solution(mesh):
    return jax.shard_map(
        shards,
        mesh=mesh,
        in_specs=(
            P("section", "tensor", None),
            P("section", "tensor", None),
            P("section", None, "tensor"),
            P("section", "tensor", None),
            P("section", None, "tensor"),
        ),
        out_specs=(
            P("section", "tensor", None),
            P("section", "tensor", None),
            P("section", None, "tensor"),
        ),
        check_vma=False,
    )
```
